512 devices in a mesh: samp: 32 (over x_hi, y, core), feat: 16 (over x_lo, z).
Axes of the slice: x: 4 (x_hi: 2, x_lo: 2; x = x_hi * 2 + x_lo), y: 8, z: 8, core: 2. Of those that a mesh axis runs over, the one named last changes fastest.
Arguments:
- labels: int32 [2097152], P('samp'), may hold values 0 or 1
- beta: float32 [1048576], P('feat'), may hold values from -1.2 to 1.2
- tile_rows: int32 [32, 16, 64], P('samp', 'feat'), may hold values from 0 to 511, as said below
- tile_cols: int32 [32, 16, 64], P('samp', 'feat'), may hold values from 0 to 511, as said below
- tile_values: bfloat16 [32, 16, 64, 128, 128], P('samp', 'feat'), may hold values from -0.5 to 0.5
- block_order: int32 [16, 16], P('feat'), may hold values from 0 to 511, as said below
- hess_inv: float32 [16, 16, 128, 128], P('feat')
Outputs:
- beta_new: float32 [1048576], P('feat')
- residual: float32 [2097152], P(('samp', 'feat'))
The draws below stay inside these ranges and needn't reach their ends.
Inputs may be any that keep to these rules, and one draw needn't show every extreme that they name: `tile_rows`: row block numbers within a samp index. `tile_cols`: feature block numbers within a feat index. Each row of block_order holds 16 distinct block numbers.
All inputs are finite; a program needn't handle non-finite values. No bound on the sum of `labels` on one device may be relied on, other than what follows from the above.
Results may differ from the reference program's by a relative error of at most 0.0025.
Values sent between devices are 32-bit elements; how exact they have to be, the bound alone decides.
A program may use at most 64 MiB of HBM per device.

```python
import jax
import jax.numpy as jnp
from jax import lax

TILE = 128
FEAT_BLOCKS = 512
GROUP_BLOCKS = 32
TILES = 64
SECTIONS = 16
ROW_BLOCKS = 512
ROWS_DEV = 65536
SAMPLES = 2097152
FEATURES = 1048576
N_SAMP = 32
N_FEAT = 16


def tile_layout(key):
    base = jax.random.fold_in(key, 11)
    key_order, key_section, key_kind, key_offset, key_col, key_row = jax.random.split(base, 6)
    samp_count = SAMPLES // ROWS_DEV
    order_keys = jax.random.split(key_order, SECTIONS)
    raw_order = jax.vmap(lambda subkey: jax.random.permutation(subkey, FEAT_BLOCKS)[:SECTIONS])(order_keys).astype(jnp.int32)
    order_rows = jnp.arange(SECTIONS, dtype=jnp.int32)
    shifting = jnp.where(order_rows == 0, FEAT_BLOCKS - 1 - raw_order[:, 0], 0)
    shifting = jnp.where(order_rows == 1, -raw_order[:, 0], shifting)
    block_order = ((raw_order + shifting[:, None]) % FEAT_BLOCKS).astype(jnp.int32)
    shape = (samp_count, SECTIONS, TILES)
    slot_ids = jnp.arange(TILES, dtype=jnp.int32)[None, None, :]
    section_pick = jax.random.randint(key_section, shape, 0, SECTIONS)
    section_pick = jnp.where(slot_ids < SECTIONS, slot_ids, section_pick).astype(jnp.int32)
    background = (jax.random.randint(key_kind, shape, 0, 2) == 1) & (slot_ids >= SECTIONS)
    feat_index = jnp.arange(SECTIONS, dtype=jnp.int32)[None, :, None]
    group_index = (feat_index - section_pick) % SECTIONS
    offsets = jax.random.randint(key_offset, shape, 0, GROUP_BLOCKS).astype(jnp.int32)
    offsets = offsets.at[0, 0, 0].set(0).at[0, SECTIONS - 1, 0].set(GROUP_BLOCKS - 1)
    row_ids = group_index * GROUP_BLOCKS + offsets
    row_ids = jnp.where(background, jax.random.randint(key_row, shape, 0, ROW_BLOCKS), row_ids)
    full_order = jnp.broadcast_to(block_order[None, :, :], (samp_count, SECTIONS, SECTIONS))
    visited = jnp.take_along_axis(full_order, section_pick, axis=2)
    col_ids = jnp.where(background, jax.random.randint(key_col, shape, 0, FEAT_BLOCKS), visited)
    return (row_ids.astype(jnp.int32), col_ids.astype(jnp.int32), block_order)


def draw_tile_rows(key, part):
    return tile_layout(key)[0]


def draw_tile_cols(key, part):
    return tile_layout(key)[1]


def draw_block_order(key, part):
    return tile_layout(key)[2]


def draw_hess_inv(key, part):
    key_diag, key_spread = jax.random.split(jax.random.fold_in(key, 23))
    shape = (SECTIONS, SECTIONS, TILE, TILE)
    diagonal = jax.random.uniform(key_diag, (SECTIONS, SECTIONS, TILE), jnp.float32, 0.05, 0.15)
    spread_part = jax.random.normal(key_spread, shape, jnp.float32)
    spread_part = spread_part * (0.033 * TILE ** (-0.5))
    identity = jnp.eye(TILE, dtype=jnp.float32)
    return spread_part * (1.0 - identity) + identity * diagonal[..., None]


def set_ends(result, rng, smallest, largest):
    spot = [jax.random.randint(jax.random.fold_in(rng, axis), (), 0, length) for axis, length in enumerate(result.shape)]
    main_axis = result.shape.index(max(result.shape))
    beside = spot[:main_axis] + [(spot[main_axis] + 1) % result.shape[main_axis]] + spot[main_axis + 1:]
    return result.at[tuple(spot)].set(smallest).at[tuple(beside)].set(largest)


def steps_of(own_key, shape, cuts, least, high):
    def one(dim, shards_of):
        steps = jax.random.uniform(jax.random.fold_in(jax.random.fold_in(own_key, 6), dim), (shards_of,), jnp.float32, least / len(cuts), high / len(cuts))
        return jnp.repeat(jnp.exp(steps), shape[dim] // shards_of).reshape((-1,) + (1,) * (len(shape) - dim - 1))

    loudness = one(*cuts[0])
    for cut in cuts[1:]:
        loudness = loudness * one(*cut)
    return loudness


def bell_draw(stream_key, extent, scale, limit, pieces=(), held_as=jnp.bfloat16):
    drawn = jax.random.normal(stream_key, extent, jnp.float32) * scale
    if len(pieces) > 0:
        drawn = steps_of(stream_key, extent, pieces, -0.22, 0.18) * drawn
    return jnp.clip(drawn, min=-limit, max=limit).astype(held_as)


def setup_inputs(seed: int = 0) -> dict:
    streams_of = jax.random.split(jax.random.key(seed), 8)
    labels = set_ends((jax.random.randint(streams_of[0], (SAMPLES,), 0, 2) < 1).astype(jnp.int32), jax.random.fold_in(streams_of[0], 1), 0, 1)
    beta = bell_draw(streams_of[1], (FEATURES,), 0.2, 1.2, ((0, 16),), jnp.float32)
    tile_rows = draw_tile_rows(jax.random.fold_in(streams_of[7], 71), 0)
    tile_cols = draw_tile_cols(jax.random.fold_in(streams_of[7], 71), 0)
    tile_values = bell_draw(streams_of[4], (N_SAMP, N_FEAT, TILES, TILE, TILE), TILE ** -0.5, 0.5, ((0, 32), (1, 16)))
    block_order = draw_block_order(jax.random.fold_in(streams_of[7], 71), 0)
    hess_inv = draw_hess_inv(jax.random.fold_in(streams_of[7], 71), 0)
    return dict(labels=labels, beta=beta, tile_rows=tile_rows, tile_cols=tile_cols, tile_values=tile_values, block_order=block_order, hess_inv=hess_inv)


exact_prec = lax.Precision.HIGHEST
l1_penalty = 0.25


def reference(labels, beta, tile_rows, tile_cols, tile_values, block_order, hess_inv):
    blocks = beta.reshape(N_FEAT, FEAT_BLOCKS, TILE)
    rounded_beta = blocks.astype(jnp.bfloat16).astype(jnp.float32)
    block_ids = jnp.arange(ROW_BLOCKS, dtype=jnp.int32)

    def margin_rows(packed):
        row_ids, col_ids, values = packed
        picked = jax.vmap(lambda table, index: table[index])(rounded_beta, col_ids)
        products = jnp.einsum("jkrc,jkc->jkr", values.astype(jnp.float32), picked, precision=exact_prec)
        placing = (row_ids[:, :, None] == block_ids[None, None, :]).astype(jnp.float32)
        partial_sum = jnp.einsum("jkb,jkr->jbr", placing, products, precision=exact_prec)
        return jnp.sum(partial_sum, axis=0)

    margins = lax.map(margin_rows, (tile_rows, tile_cols, tile_values))
    probability = jax.nn.sigmoid(margins)
    weight = (probability * (1.0 - probability)).reshape(N_SAMP, N_FEAT, GROUP_BLOCKS, TILE)
    residual = (labels.reshape(N_SAMP, ROW_BLOCKS, TILE).astype(jnp.float32) - probability).reshape(N_SAMP, N_FEAT, GROUP_BLOCKS, TILE)
    feat_ids = jnp.arange(N_FEAT, dtype=jnp.int32)
    sub_ids = jnp.arange(GROUP_BLOCKS, dtype=jnp.int32)
    for section_index in range(SECTIONS):
        groups = (feat_ids - section_index) % N_FEAT
        targets = block_order[:, section_index]
        inverses = hess_inv[:, section_index]

        def choose(row_ids, col_ids):
            offsets = row_ids - groups[:, None] * GROUP_BLOCKS
            matches = (col_ids == targets[:, None]) & (offsets >= 0) & (offsets < GROUP_BLOCKS)
            return ((offsets[:, :, None] == sub_ids[None, None, :]) & matches[:, :, None]).astype(jnp.float32)

        def gradient_part(packed):
            row_ids, col_ids, values, part_resid = packed
            chosen = choose(row_ids, col_ids)
            rounded = lax.optimization_barrier(part_resid[groups].astype(jnp.bfloat16)).astype(jnp.float32)
            resid_tiles = jnp.einsum("jkg,jgt->jkt", chosen, rounded, precision=exact_prec)
            return jnp.einsum("jkrc,jkr->jc", values.astype(jnp.float32), resid_tiles, precision=exact_prec)

        gradient = jnp.sum(lax.map(gradient_part, (tile_rows, tile_cols, tile_values, residual)), axis=0)
        current = blocks[feat_ids, targets]
        moved_block = current + jnp.einsum("jab,jb->ja", inverses, gradient, precision=exact_prec)
        shrunk = jnp.sign(moved_block) * jnp.maximum(jnp.abs(moved_block) - l1_penalty, 0.0)
        change = lax.optimization_barrier((shrunk - current).astype(jnp.bfloat16)).astype(jnp.float32)
        blocks = blocks.at[feat_ids, targets].set(shrunk)

        def update_part(packed):
            row_ids, col_ids, values, part_resid, part_weight = packed
            chosen = choose(row_ids, col_ids)
            image_rows = jnp.einsum("jkrc,jc->jkr", values.astype(jnp.float32), change, precision=exact_prec)
            landed = jnp.einsum("jkg,jkr->jgr", chosen, image_rows, precision=exact_prec)
            return part_resid.at[groups].set(part_resid[groups] - part_weight[groups] * landed)

        residual = lax.map(update_part, (tile_rows, tile_cols, tile_values, residual, weight))
    return blocks.reshape(-1), residual.reshape(-1)
```

```python
import functools

import jax
import jax.numpy as jnp
from jax import lax
from jax.experimental import pallas as pl
from jax.experimental.pallas import tpu as pltpu
from jax.sharding import PartitionSpec as P

MESH = pl.DeviceIdType.MESH
EXACT = lax.Precision.HIGHEST
L1 = 0.25
SLAB = 16


def nt_dot(a, b, precision=None):
    return lax.dot_general(
        a, b, (((1,), (1,)), ((), ())), precision=precision, preferred_element_type=jnp.float32
    )


def window_kernel(
    n_samp,
    n_feat,
    n_tiles,
    rows_ref,
    cols_ref,
    cols_smem,
    order_smem,
    labels_hbm,
    beta_hbm,
    vals_hbm,
    hess_hbm,
    beta_out,
    res_out,
    labels_v,
    beta_v,
    vals,
    hess,
    ids,
    partial,
    m_recv,
    g_send,
    g_recv,
    r_send,
    r_buf,
    w_buf,
    shrunk_all,
    load_sem,
    m_send_sem,
    m_recv_sem,
    g_send_sem,
    g_recv_sem,
    r_send_sem,
    r_recv_sem,
    w_send_sem,
    w_recv_sem,
):
    si = lax.axis_index("samp")
    fj = lax.axis_index("feat")
    group = labels_v.shape[0]
    edge = vals.shape[-1]
    right = lax.rem(fj + 1, n_feat)

    own_rows = pl.ds(pl.multiple_of(fj * group, group), group)
    loads = [
        pltpu.make_async_copy(vals_hbm, vals, load_sem.at[0]),
        pltpu.make_async_copy(beta_hbm, beta_v, load_sem.at[1]),
        pltpu.make_async_copy(labels_hbm.at[own_rows], labels_v, load_sem.at[2]),
        pltpu.make_async_copy(hess_hbm, hess, load_sem.at[3]),
    ]
    for load in loads:
        load.start()

    barrier = pltpu.get_barrier_semaphore()
    for d in range(1, n_samp):
        pl.semaphore_signal(
            barrier, inc=1, device_id=(lax.rem(si + d, n_samp), fj), device_id_type=MESH
        )
    for d in range(1, n_feat):
        pl.semaphore_signal(
            barrier, inc=1, device_id=(si, lax.rem(fj + d, n_feat)), device_id_type=MESH
        )

    ids[...] = jnp.full(ids.shape, -1, jnp.int32)
    ids[0:1, 0:n_tiles] = rows_ref[...]
    ids[1:2, 0:n_tiles] = cols_ref[...]
    row_id = ids[0:1, :]
    col_id = ids[1:2, :]
    tile_section = lax.rem(fj - lax.shift_right_arithmetic(row_id, group.bit_length() - 1) + 2 * n_feat, n_feat)
    offset_row = jnp.bitwise_and(row_id, group - 1)
    section_row = jnp.full(row_id.shape, -1, jnp.int32)
    for s in range(n_feat):
        hit = (tile_section == s) & (col_id == order_smem[0, s])
        section_row = jnp.where(hit, s, section_row)
    offset_col = jnp.transpose(jnp.broadcast_to(offset_row, (edge, edge)))[:n_tiles, :group]
    section_col = jnp.transpose(jnp.broadcast_to(section_row, (edge, edge)))[:n_tiles, :group]
    offset_row = jnp.broadcast_to(offset_row[:, :n_tiles], (group, n_tiles))
    section_row = jnp.broadcast_to(section_row[:, :n_tiles], (group, n_tiles))
    same_col = offset_col == lax.broadcasted_iota(jnp.int32, (n_tiles, group), 1)
    same_row = offset_row == lax.broadcasted_iota(jnp.int32, (group, n_tiles), 0)
    sub = lax.broadcasted_iota(jnp.int32, (SLAB, edge), 0)
    slabs = n_tiles // SLAB

    def tile_images(lhs):
        out = []
        for m in range(slabs):
            acc = jnp.zeros((SLAB, edge), jnp.float32)
            for t in range(SLAB):
                acc = jnp.where(sub == t, nt_dot(lhs[m], vals[m * SLAB + t]), acc)
            out.append(acc)
        return jnp.concatenate(out, axis=0)

    loads[0].wait()
    loads[1].wait()
    picked = []
    for m in range(slabs):
        acc = jnp.zeros((SLAB, edge), jnp.float32)
        for t in range(SLAB):
            row = beta_v[pl.ds(cols_smem[0, m * SLAB + t], 1), :]
            acc = jnp.where(sub == t, jnp.broadcast_to(row, (SLAB, edge)), acc)
        picked.append(acc.astype(jnp.bfloat16))
    products = tile_images(picked)
    row_blocks = partial.shape[0] * group
    placing = jnp.broadcast_to(ids[0:1, 0:n_tiles], (row_blocks, n_tiles)) == lax.broadcasted_iota(
        jnp.int32, (row_blocks, n_tiles), 0
    )
    sums = jnp.dot(placing.astype(jnp.float32), products, precision=EXACT)
    partial[...] = sums.reshape(partial.shape)

    pl.semaphore_wait(barrier, n_samp + n_feat - 2)
    for d in range(1, n_feat):
        peer = lax.rem(fj + d, n_feat)
        pltpu.make_async_remote_copy(
            src_ref=partial.at[peer],
            dst_ref=m_recv.at[fj],
            send_sem=m_send_sem,
            recv_sem=m_recv_sem,
            device_id=(si, peer),
            device_id_type=MESH,
        ).start()
    m_recv[fj] = partial[fj]
    fifteen = m_recv.at[pl.ds(0, n_feat - 1)]
    pltpu.make_async_copy(fifteen, fifteen, m_recv_sem).wait()
    margin = m_recv[0]
    for d in range(1, n_feat):
        margin = margin + m_recv[d]
    prob = 1.0 / (1.0 + jnp.exp(-margin))
    loads[2].wait()
    w_buf[0] = prob * (1.0 - prob)
    r_buf[0] = labels_v[...].astype(jnp.float32) - prob

    def shift(buf_src, buf_dst, send_sem, recv_sem):
        return pltpu.make_async_remote_copy(
            src_ref=buf_src,
            dst_ref=buf_dst,
            send_sem=send_sem,
            recv_sem=recv_sem,
            device_id=(si, right),
            device_id_type=MESH,
        )

    shift(w_buf.at[0], w_buf.at[1], w_send_sem, w_recv_sem.at[1]).start()
    loads[3].wait()

    def section(s, carry):
        residual = r_buf[s]
        chosen = (same_col & (section_col == s)).astype(jnp.bfloat16)
        tiles = jnp.dot(
            chosen, residual.astype(jnp.bfloat16), preferred_element_type=jnp.float32
        ).astype(jnp.bfloat16)
        lhs = []
        for k in range(n_tiles):
            m, t = k // SLAB, k % SLAB
            lhs.append(
                jnp.where(sub == t, tiles[m * SLAB : (m + 1) * SLAB], jnp.zeros((), jnp.bfloat16))
            )
        grads = jnp.dot(
            jnp.concatenate(lhs, axis=1),
            vals[...].reshape(n_tiles * edge, edge),
            preferred_element_type=jnp.float32,
        )
        local = jnp.sum(grads, axis=0, keepdims=True)
        g_send[s] = local
        for d in list(range(1, n_samp)):
            pltpu.make_async_remote_copy(
                src_ref=g_send.at[s],
                dst_ref=g_recv.at[s, si],
                send_sem=g_send_sem,
                recv_sem=g_recv_sem.at[s],
                device_id=(lax.rem(si + d, n_samp), fj),
                device_id_type=MESH,
            ).start()
        g_recv[s, si] = local

        @pl.when(s < n_feat - 1)
        def _():
            shift(w_buf.at[s], w_buf.at[s + 1], w_send_sem, w_recv_sem.at[s + 1]).wait_recv()

        @pl.when(s < n_feat - 2)
        def _():
            shift(w_buf.at[s + 1], w_buf.at[s + 2], w_send_sem, w_recv_sem.at[s + 2]).start()

        current = beta_v[pl.ds(order_smem[0, s], 1), :]
        others = g_recv.at[s, pl.ds(0, n_samp - 1)]
        pltpu.make_async_copy(others, others, g_recv_sem.at[s]).wait()
        gradient = g_recv[s, 0]
        for i in range(1, n_samp):
            gradient = gradient + g_recv[s, i]
        step = nt_dot(jnp.broadcast_to(gradient, (8, edge)), hess[s], EXACT)[0:1, :]
        moved = current + step
        shrunk = jnp.where(moved > L1, moved - L1, jnp.where(moved < -L1, moved + L1, 0.0))
        shrunk_all[s] = shrunk
        change = jnp.broadcast_to(shrunk - current, (SLAB, edge)).astype(jnp.bfloat16)
        image = tile_images([change] * slabs)
        chosen_t = (same_row & (section_row == s)).astype(jnp.float32)
        landed = jnp.dot(chosen_t, image, precision=EXACT)
        r_send[s] = residual - w_buf[s] * landed
        copy = shift(r_send.at[s], r_buf.at[s + 1], r_send_sem, r_recv_sem.at[s + 1])
        copy.start()
        copy.wait_recv()
        return carry

    lax.fori_loop(0, n_feat, section, 0)

    res_out[...] = r_buf[n_feat]
    blocks = beta_v[...]
    block_ids = lax.broadcasted_iota(jnp.int32, blocks.shape, 0)
    for s in range(n_feat):
        blocks = jnp.where(
            block_ids == order_smem[0, s], jnp.broadcast_to(shrunk_all[s], blocks.shape), blocks
        )
    beta_out[...] = blocks

    pltpu.make_async_copy(fifteen, fifteen, m_send_sem).wait()
    sent = g_recv.at[:, pl.ds(0, n_samp - 1)]
    pltpu.make_async_copy(sent, sent, g_send_sem).wait()
    sent_r = r_buf.at[pl.ds(0, n_feat)]
    pltpu.make_async_copy(sent_r, sent_r, r_send_sem).wait()
    sent_w = w_buf.at[pl.ds(0, n_feat - 1)]
    pltpu.make_async_copy(sent_w, sent_w, w_send_sem).wait()


def per_device(n_samp, n_feat, labels, beta, tile_rows, tile_cols, tile_values, block_order, hess_inv):
    n_tiles, edge = tile_values.shape[2], tile_values.shape[-1]
    row_blocks = labels.shape[0] // edge
    feat_blocks = beta.shape[0] // edge
    group = row_blocks // n_feat
    vmem = pl.BlockSpec(memory_space=pltpu.VMEM)
    smem = pl.BlockSpec(memory_space=pltpu.SMEM)
    anywhere = pl.BlockSpec(memory_space=pl.ANY)
    f32 = jnp.float32
    dma = pltpu.SemaphoreType.DMA
    rows = tile_rows.reshape(1, n_tiles)
    cols = tile_cols.reshape(1, n_tiles)
    beta_new, residual = pl.pallas_call(
        functools.partial(window_kernel, n_samp, n_feat, n_tiles),
        out_shape=(
            jax.ShapeDtypeStruct((feat_blocks, edge), f32),
            jax.ShapeDtypeStruct((group, edge), f32),
        ),
        in_specs=[vmem, vmem, smem, smem, anywhere, anywhere, anywhere, anywhere],
        out_specs=(vmem, vmem),
        scratch_shapes=[
            pltpu.VMEM((group, edge), jnp.int32),
            pltpu.VMEM((feat_blocks, edge), f32),
            pltpu.VMEM((n_tiles, edge, edge), jnp.bfloat16),
            pltpu.VMEM((n_feat, edge, edge), f32),
            pltpu.VMEM((8, edge), jnp.int32),
            pltpu.VMEM((n_feat, group, edge), f32),
            pltpu.VMEM((n_feat, group, edge), f32),
            pltpu.VMEM((n_feat, 1, edge), f32),
            pltpu.VMEM((n_feat, n_samp, 1, edge), f32),
            pltpu.VMEM((n_feat, group, edge), f32),
            pltpu.VMEM((n_feat + 1, group, edge), f32),
            pltpu.VMEM((n_feat, group, edge), f32),
            pltpu.VMEM((n_feat, 1, edge), f32),
            dma((4,)),
            dma(()),
            dma(()),
            dma(()),
            dma((n_feat,)),
            dma(()),
            dma((n_feat + 1,)),
            dma(()),
            dma((n_feat,)),
        ],
        compiler_params=pltpu.CompilerParams(collective_id=0, has_side_effects=True),
    )(
        rows,
        cols,
        cols,
        block_order,
        labels.reshape(row_blocks, edge),
        beta.reshape(feat_blocks, edge),
        tile_values.reshape(n_tiles, edge, edge),
        hess_inv.reshape(n_feat, edge, edge),
    )
    return beta_new.reshape(-1), residual.reshape(-1)


def solution(mesh):
    placed = (
        P("samp"),
        P("feat"),
        P("samp", "feat", None),
        P("samp", "feat", None),
        P("samp", "feat", None, None, None),
        P("feat", None),
        P("feat", None, None, None),
    )
    return jax.shard_map(
        functools.partial(per_device, mesh.shape["samp"], mesh.shape["feat"]),
        mesh=mesh,
        in_specs=placed,
        out_specs=(P("feat"), P(("samp", "feat"))),
        check_vma=False,
    )
```

```python
import functools

import jax
import jax.numpy as jnp
from jax import lax
from jax.experimental import pallas as pl
from jax.experimental.pallas import tpu as pltpu
from jax.sharding import PartitionSpec as P

MESH = pl.DeviceIdType.MESH
L1 = 0.25
SLAB = 16
BF16 = jnp.bfloat16
F32 = jnp.float32


def nt_dot(a, b):
    return lax.dot_general(a, b, (((1,), (1,)), ((), ())), preferred_element_type=F32)


def three_parts(x):
    high = x.astype(BF16)
    rest = x - high.astype(F32)
    middle = rest.astype(BF16)
    low = (rest - middle.astype(F32)).astype(BF16)
    return high, middle, low


def tree_sum(terms):
    while len(terms) > 1:
        terms = [a + b for a, b in zip(terms[::2], terms[1::2])] + terms[len(terms) // 2 * 2 :]
    return terms[0]


def window_kernel(
    n_samp,
    n_feat,
    n_tiles,
    rows_ref,
    cols_ref,
    cols_smem,
    order_smem,
    labels_hbm,
    beta_hbm,
    vals_hbm,
    hess_hbm,
    beta_out,
    res_out,
    labels_v,
    vals,
    hess,
    hess_t,
    ids,
    index_v,
    index_s,
    prefix,
    prefix_t,
    dense,
    dense_t,
    shrunk_all,
    partial,
    m_recv,
    g_send,
    g_recv,
    r_send,
    r_buf,
    w_buf,
    load_sem,
    index_sem,
    m_send_sem,
    m_recv_sem,
    g_send_sem,
    g_recv_sem,
    r_send_sem,
    r_recv_sem,
    w_send_sem,
    w_recv_sem,
):
    si = lax.axis_index("samp")
    fj = lax.axis_index("feat")
    group = labels_v.shape[0]
    shift_bits = group.bit_length() - 1
    edge = vals.shape[-1]
    slabs = n_tiles // SLAB
    right = lax.rem(fj + 1, n_feat)
    row_blocks = n_feat * group
    starts = row_blocks + edge

    own_rows = pl.ds(pl.multiple_of(fj * group, group), group)
    loads = [
        pltpu.make_async_copy(vals_hbm, vals, load_sem.at[0]),
        pltpu.make_async_copy(beta_hbm, beta_out, load_sem.at[1]),
        pltpu.make_async_copy(labels_hbm.at[own_rows], labels_v, load_sem.at[2]),
        pltpu.make_async_copy(hess_hbm, hess, load_sem.at[3]),
    ]
    for load in loads:
        load.start()

    barrier = pltpu.get_barrier_semaphore()
    for d in range(1, n_samp):
        pl.semaphore_signal(
            barrier, inc=1, device_id=(lax.rem(si + d, n_samp), fj), device_id_type=MESH
        )
    for d in range(1, n_feat):
        pl.semaphore_signal(
            barrier, inc=1, device_id=(si, lax.rem(fj + d, n_feat)), device_id_type=MESH
        )

    last = 2 * row_blocks
    ids[...] = jnp.full(ids.shape, -1, jnp.int32)
    ids[0:1, 0:n_tiles] = rows_ref[...]
    ids[1:2, 0:n_tiles] = cols_ref[...]
    row_id, col_id = ids[0:1, :], ids[1:2, :]
    section = lax.rem(fj - lax.shift_right_arithmetic(row_id, shift_bits) + 2 * n_feat, n_feat)
    code = jnp.full(row_id.shape, last, jnp.int32)
    for s in range(n_feat):
        hit = (section == s) & (col_id == order_smem[0, s])
        code = jnp.where(hit, s * group + jnp.bitwise_and(row_id, group - 1), code)

    def down(row):
        return jnp.transpose(jnp.broadcast_to(row, (edge, edge)))

    lane = lax.broadcasted_iota(jnp.int32, (1, edge), 1)
    across = lax.broadcasted_iota(jnp.int32, (edge, edge), 1)
    along = lax.broadcasted_iota(jnp.int32, (edge, edge), 0)
    code_down = down(code)
    for b in range(starts // edge):
        before = (code_down < across + b * edge).astype(jnp.int32)
        index_v[0:1, b * edge : (b + 1) * edge] = jnp.sum(before, axis=0, keepdims=True)
    key = code * edge + lane
    rank = jnp.sum((down(key) < key).astype(jnp.int32), axis=0, keepdims=True)
    index_v[0:1, starts : starts + edge] = jnp.sum(
        jnp.where(down(rank) == across, along, 0), axis=0, keepdims=True
    )
    index_copy = pltpu.make_async_copy(index_v, index_s, index_sem)
    index_copy.start()

    sub = lax.broadcasted_iota(jnp.int32, (SLAB, edge), 0)
    row_is = [(sub == t).astype(F32).astype(BF16) for t in range(SLAB)]

    def set_prefixes():
        prefix[0] = jnp.zeros((edge, edge), F32)
        prefix_t[0] = jnp.zeros((edge, edge), F32)
        eye = (along == across).astype(F32).astype(BF16)

        def add_tile(n, carry):
            tile = vals[index_s[0, starts + n]]
            prefix[n + 1] = prefix[n] + tile.astype(F32)
            prefix_t[n + 1] = prefix_t[n] + nt_dot(eye, tile)
            return carry

        lax.fori_loop(0, n_tiles, add_tile, 0)

    def set_dense(s, source, out):
        for g in range(group):
            at = s * group + g
            out[g] = (source[index_s[0, at + 1]] - source[index_s[0, at]]).astype(BF16)

    def set_hessian(s):
        for p, part in enumerate(three_parts(jnp.transpose(hess[s]))):
            hess_t[pl.ds(p * edge, edge)] = part

    def set_block(s):
        blocks = beta_out[...]
        block_ids = lax.broadcasted_iota(jnp.int32, blocks.shape, 0)
        beta_out[...] = jnp.where(
            block_ids == order_smem[0, s], jnp.broadcast_to(shrunk_all[s], blocks.shape), blocks
        )

    loads[0].wait()
    loads[1].wait()
    products = []
    for m in range(slabs):
        acc = jnp.zeros((SLAB, edge), F32)
        for t in range(SLAB):
            row = beta_out[pl.ds(cols_smem[0, m * SLAB + t], 1), :]
            acc = jnp.where(sub == t, jnp.broadcast_to(row, (SLAB, edge)), acc)
        picked = acc.astype(BF16)
        acc = jnp.zeros((SLAB, edge), F32)
        for t in range(SLAB):
            acc = jnp.where(sub == t, nt_dot(picked, vals[m * SLAB + t]), acc)
        products.append(acc)
    placing = (
        jnp.broadcast_to(ids[0:1, 0:n_tiles], (row_blocks, n_tiles))
        == lax.broadcasted_iota(jnp.int32, (row_blocks, n_tiles), 0)
    ).astype(F32).astype(BF16)
    parts = three_parts(jnp.concatenate(products, axis=0))
    sums = jnp.dot(placing, parts[0], preferred_element_type=F32)
    for part in parts[1:]:
        sums = sums + jnp.dot(placing, part, preferred_element_type=F32)
    partial[...] = sums.reshape(partial.shape)

    pl.semaphore_wait(barrier, n_samp + n_feat - 2)
    for d in [x for y in range(n_feat // 2, 0, -1) for x in sorted({y, n_feat - y})]:
        peer = lax.rem(fj + d, n_feat)
        pltpu.make_async_remote_copy(
            src_ref=partial.at[peer],
            dst_ref=m_recv.at[fj],
            send_sem=m_send_sem,
            recv_sem=m_recv_sem,
            device_id=(si, peer),
            device_id_type=MESH,
        ).start()
    m_recv[fj] = partial[fj]
    loads[2].wait()
    loads[3].wait()
    set_hessian(0)
    index_copy.wait()
    set_prefixes()
    set_dense(0, prefix, dense)
    set_dense(0, prefix_t, dense_t)
    fifteen = m_recv.at[pl.ds(0, n_feat - 1)]
    pltpu.make_async_copy(fifteen, fifteen, m_recv_sem).wait()
    margin = tree_sum([m_recv[d] for d in range(n_feat)])
    prob = 1.0 / (1.0 + jnp.exp(-margin))
    w_buf[0] = prob * (1.0 - prob)
    r_buf[0] = labels_v[...].astype(F32) - prob

    def shift(buf_src, buf_dst, send_sem, recv_sem):
        return pltpu.make_async_remote_copy(
            src_ref=buf_src,
            dst_ref=buf_dst,
            send_sem=send_sem,
            recv_sem=recv_sem,
            device_id=(si, right),
            device_id_type=MESH,
        )

    shift(w_buf.at[0], w_buf.at[1], w_send_sem, w_recv_sem.at[1]).start()

    peers = sorted(
        ((x, y, c) for x in range(2) for y in range(n_samp // 4) for c in range(2)),
        key=lambda o: -(2 * o[0] + min(o[1], n_samp // 4 - o[1]) + 0.3 * o[2]),
    )[:-1]
    half = n_samp // 2
    my_x, my_y, my_c = si // half, lax.rem(si // 2, n_samp // 4), lax.rem(si, 2)

    def section(s, carry):
        rounded = r_buf[s].astype(BF16)
        picks = jnp.concatenate(
            [
                row_is[g % SLAB] * rounded[g // SLAB * SLAB : (g // SLAB + 1) * SLAB]
                for g in range(group)
            ],
            axis=1,
        )
        grads = jnp.dot(picks, dense[...].reshape(group * edge, edge), preferred_element_type=F32)
        local = jnp.sum(grads, axis=0, keepdims=True)
        g_send[s] = local
        for dx, dy, dc in peers:
            peer = (
                lax.rem(my_x + dx, 2) * half
                + lax.rem(my_y + dy, n_samp // 4) * 2
                + lax.rem(my_c + dc, 2)
            )
            pltpu.make_async_remote_copy(
                src_ref=g_send.at[s],
                dst_ref=g_recv.at[s, si],
                send_sem=g_send_sem,
                recv_sem=g_recv_sem.at[s],
                device_id=(peer, fj),
                device_id_type=MESH,
            ).start()
        g_recv[s, si] = local

        @pl.when(s < n_feat - 1)
        def _():
            shift(w_buf.at[s], w_buf.at[s + 1], w_send_sem, w_recv_sem.at[s + 1]).wait_recv()
            set_dense(s + 1, prefix, dense)

        @pl.when(s > 0)
        def _():
            set_block(s - 1)

        @pl.when(s < n_feat - 2)
        def _():
            shift(w_buf.at[s + 1], w_buf.at[s + 2], w_send_sem, w_recv_sem.at[s + 2]).start()

        target = order_smem[0, s]
        current = beta_out[pl.ds(target, 1), :]
        others = g_recv.at[s, pl.ds(0, n_samp - 1)]
        pltpu.make_async_copy(others, others, g_recv_sem.at[s]).wait()
        gradient = tree_sum([g_recv[s, i] for i in range(n_samp)])
        high, middle, low = [
            jnp.broadcast_to(part.astype(F32), (SLAB, edge)) for part in three_parts(gradient)
        ]
        stacked = jnp.where(
            sub == 0, high, jnp.where(sub == 1, middle, jnp.where(sub == 2, low, 0.0))
        ).astype(BF16)
        products = jnp.dot(
            jnp.concatenate([stacked] * 3, axis=1), hess_t[...], preferred_element_type=F32
        )
        moved = current + jnp.sum(products, axis=0, keepdims=True)
        shrunk = jnp.where(moved > L1, moved - L1, jnp.where(moved < -L1, moved + L1, 0.0))
        shrunk_all[s] = shrunk
        change = jnp.broadcast_to(shrunk - current, (SLAB, edge)).astype(BF16)
        spread = jnp.concatenate([row_is[t] * change for t in range(SLAB)], axis=1)
        landed = jnp.concatenate(
            [
                jnp.dot(
                    spread,
                    dense_t[pl.ds(m * SLAB, SLAB)].reshape(SLAB * edge, edge),
                    preferred_element_type=F32,
                )
                for m in range(group // SLAB)
            ],
            axis=0,
        )
        r_send[s] = r_buf[s] - w_buf[s] * landed
        copy = shift(r_send.at[s], r_buf.at[s + 1], r_send_sem, r_recv_sem.at[s + 1])
        copy.start()

        @pl.when(s < n_feat - 1)
        def _():
            set_hessian(s + 1)
            set_dense(s + 1, prefix_t, dense_t)

        copy.wait_recv()
        return carry

    lax.fori_loop(0, n_feat, section, 0)

    set_block(n_feat - 1)
    res_out[...] = r_buf[n_feat]

    pltpu.make_async_copy(fifteen, fifteen, m_send_sem).wait()
    sent = g_recv.at[:, pl.ds(0, n_samp - 1)]
    pltpu.make_async_copy(sent, sent, g_send_sem).wait()
    sent_r = r_buf.at[pl.ds(0, n_feat)]
    pltpu.make_async_copy(sent_r, sent_r, r_send_sem).wait()
    sent_w = w_buf.at[pl.ds(0, n_feat - 1)]
    pltpu.make_async_copy(sent_w, sent_w, w_send_sem).wait()


def per_device(n_samp, n_feat, labels, beta, tile_rows, tile_cols, tile_values, block_order, hess_inv):
    n_tiles, edge = tile_values.shape[2], tile_values.shape[-1]
    row_blocks = labels.shape[0] // edge
    feat_blocks = beta.shape[0] // edge
    group = row_blocks // n_feat
    vmem = pl.BlockSpec(memory_space=pltpu.VMEM)
    smem = pl.BlockSpec(memory_space=pltpu.SMEM)
    anywhere = pl.BlockSpec(memory_space=pl.ANY)
    dma = pltpu.SemaphoreType.DMA
    beta_new, residual = pl.pallas_call(
        functools.partial(window_kernel, n_samp, n_feat, n_tiles),
        out_shape=(
            jax.ShapeDtypeStruct((feat_blocks, edge), F32),
            jax.ShapeDtypeStruct((group, edge), F32),
        ),
        in_specs=[vmem, vmem, smem, smem, anywhere, anywhere, anywhere, anywhere],
        out_specs=(vmem, vmem),
        scratch_shapes=[
            pltpu.VMEM((group, edge), jnp.int32),
            pltpu.VMEM((n_tiles, edge, edge), BF16),
            pltpu.VMEM((n_feat, edge, edge), F32),
            pltpu.VMEM((3 * edge, edge), BF16),
            pltpu.VMEM((8, edge), jnp.int32),
            pltpu.VMEM((1, row_blocks + 2 * edge), jnp.int32),
            pltpu.SMEM((1, row_blocks + 2 * edge), jnp.int32),
            pltpu.VMEM((n_tiles + 1, edge, edge), F32),
            pltpu.VMEM((n_tiles + 1, edge, edge), F32),
            pltpu.VMEM((group, edge, edge), BF16),
            pltpu.VMEM((group, edge, edge), BF16),
            pltpu.VMEM((n_feat, 1, edge), F32),
            pltpu.VMEM((n_feat, group, edge), F32),
            pltpu.VMEM((n_feat, group, edge), F32),
            pltpu.VMEM((n_feat, 1, edge), F32),
            pltpu.VMEM((n_feat, n_samp, 1, edge), F32),
            pltpu.VMEM((n_feat, group, edge), F32),
            pltpu.VMEM((n_feat + 1, group, edge), F32),
            pltpu.VMEM((n_feat, group, edge), F32),
            dma((4,)),
            dma(()),
            dma(()),
            dma(()),
            dma(()),
            dma((n_feat,)),
            dma(()),
            dma((n_feat + 1,)),
            dma(()),
            dma((n_feat,)),
        ],
        compiler_params=pltpu.CompilerParams(collective_id=0, has_side_effects=True),
    )(
        tile_rows.reshape(1, n_tiles),
        tile_cols.reshape(1, n_tiles),
        tile_cols.reshape(1, n_tiles),
        block_order,
        labels.reshape(row_blocks, edge),
        beta.reshape(feat_blocks, edge),
        tile_values.reshape(n_tiles, edge, edge),
        hess_inv.reshape(n_feat, edge, edge),
    )
    return beta_new.reshape(-1), residual.reshape(-1)


def solution(mesh):
    placed = (
        P("samp"),
        P("feat"),
        P("samp", "feat", None),
        P("samp", "feat", None),
        P("samp", "feat", None, None, None),
        P("feat", None),
        P("feat", None, None, None),
    )
    return jax.shard_map(
        functools.partial(per_device, mesh.shape["samp"], mesh.shape["feat"]),
        mesh=mesh,
        in_specs=placed,
        out_specs=(P("feat"), P(("samp", "feat"))),
        check_vma=False,
    )
```

```python
import functools

import jax
import jax.numpy as jnp
from jax import lax
from jax.experimental import pallas as pl
from jax.experimental.pallas import tpu as pltpu
from jax.sharding import PartitionSpec as P

MESH = pl.DeviceIdType.MESH
L1 = 0.25
UNROLL = 8
SLAB = 16
BF16 = jnp.bfloat16
F32 = jnp.float32


def nt_dot(a, b):
    return lax.dot_general(a, b, (((1,), (1,)), ((), ())), preferred_element_type=F32)


def three_parts(x):
    high = x.astype(BF16)
    rest = x - high.astype(F32)
    middle = rest.astype(BF16)
    low = (rest - middle.astype(F32)).astype(BF16)
    return high, middle, low


def two_dots(a, b_ref):
    half = b_ref.shape[0] // 2
    return [
        jnp.dot(a[:, rows], b_ref[rows], preferred_element_type=F32)
        for rows in (slice(0, half), slice(half, 2 * half))
    ]


def tree_sum(terms):
    while len(terms) > 1:
        terms = [a + b for a, b in zip(terms[::2], terms[1::2])] + terms[len(terms) // 2 * 2 :]
    return terms[0]


def window_kernel(
    n_samp,
    n_feat,
    n_tiles,
    rows_ref,
    cols_ref,
    cols_smem,
    order_smem,
    labels_hbm,
    beta_hbm,
    vals_hbm,
    hess_hbm,
    beta_out,
    res_out,
    labels_v,
    beta_v,
    vals,
    hess,
    hess_t,
    ids,
    index_v,
    index_s,
    prefix,
    prefix_t,
    dense,
    dense_t,
    shrunk_all,
    partial,
    x_recv,
    m_send,
    m_recv,
    g_send,
    g_recv,
    r_send,
    r_buf,
    w_buf,
    load_sem,
    index_sem,
    x_send_sem,
    x_recv_sem,
    m_send_sem,
    m_recv_sem,
    g_send_sem,
    g_recv_sem,
    r_send_sem,
    r_recv_sem,
    w_send_sem,
    w_recv_sem,
):
    si = lax.axis_index("samp")
    fj = lax.axis_index("feat")
    group = labels_v.shape[0]
    shift_bits = group.bit_length() - 1
    edge = vals.shape[-1]
    slabs = n_tiles // SLAB
    right = lax.rem(fj + 1, n_feat)
    row_blocks = n_feat * group
    starts = row_blocks + edge

    own_rows = pl.ds(pl.multiple_of(fj * group, group), group)
    loads = [
        pltpu.make_async_copy(vals_hbm, vals, load_sem.at[0]),
        pltpu.make_async_copy(beta_hbm, beta_v, load_sem.at[1]),
        pltpu.make_async_copy(labels_hbm.at[own_rows], labels_v, load_sem.at[2]),
        pltpu.make_async_copy(hess_hbm, hess, load_sem.at[3]),
    ]
    for load in loads:
        load.start()

    barrier = pltpu.get_barrier_semaphore()
    for d in range(1, n_samp):
        pl.semaphore_signal(
            barrier, inc=1, device_id=(lax.rem(si + d, n_samp), fj), device_id_type=MESH
        )
    for d in range(1, n_feat):
        pl.semaphore_signal(
            barrier, inc=1, device_id=(si, lax.rem(fj + d, n_feat)), device_id_type=MESH
        )

    last = 2 * row_blocks
    ids[...] = jnp.full(ids.shape, -1, jnp.int32)
    ids[0:1, 0:n_tiles] = rows_ref[...]
    ids[1:2, 0:n_tiles] = cols_ref[...]
    row_id, col_id = ids[0:1, :], ids[1:2, :]
    section = lax.rem(fj - lax.shift_right_arithmetic(row_id, shift_bits) + 2 * n_feat, n_feat)
    code = jnp.full(row_id.shape, last, jnp.int32)
    for s in range(n_feat):
        hit = (section == s) & (col_id == order_smem[0, s])
        code = jnp.where(hit, s * group + jnp.bitwise_and(row_id, group - 1), code)

    def down(row):
        return jnp.transpose(jnp.broadcast_to(row, (edge, edge)))

    lane = lax.broadcasted_iota(jnp.int32, (1, edge), 1)
    across = lax.broadcasted_iota(jnp.int32, (edge, edge), 1)
    along = lax.broadcasted_iota(jnp.int32, (edge, edge), 0)
    code_down = down(code)
    for b in range(starts // edge):
        before = (code_down < across + b * edge).astype(jnp.int32)
        index_v[0:1, b * edge : (b + 1) * edge] = jnp.sum(before, axis=0, keepdims=True)
    key = code * edge + lane
    rank = jnp.sum((down(key) < key).astype(jnp.int32), axis=0, keepdims=True)
    index_v[0:1, starts : starts + edge] = jnp.sum(
        jnp.where(down(rank) == across, along, 0), axis=0, keepdims=True
    )
    index_copy = pltpu.make_async_copy(index_v, index_s, index_sem)
    index_copy.start()

    sub = lax.broadcasted_iota(jnp.int32, (SLAB, edge), 0)
    row_is = [(sub == t).astype(F32).astype(BF16) for t in range(SLAB)]
    group_is = [jnp.concatenate([mask] * (group // SLAB), axis=0) for mask in row_is]

    def set_prefixes():
        prefix[0] = jnp.zeros((edge, edge), F32)
        prefix_t[0] = jnp.zeros((edge, edge), F32)
        eye = (along == across).astype(F32).astype(BF16)

        def add_tiles(b, carry):
            sums, sums_t = prefix[b * UNROLL], prefix_t[b * UNROLL]
            for u in range(UNROLL):
                n = b * UNROLL + u
                tile = vals[index_s[0, starts + n]]
                sums = sums + tile.astype(F32)
                sums_t = sums_t + nt_dot(eye, tile)
                prefix[n + 1] = sums
                prefix_t[n + 1] = sums_t
            return carry

        lax.fori_loop(0, n_tiles // UNROLL, add_tiles, 0)

    def set_dense(s, source, out):
        for g in range(group):
            at = s * group + g
            half, t = g // SLAB, g % SLAB
            out[t * edge : (t + 1) * edge, half * edge : (half + 1) * edge] = (
                source[index_s[0, at + 1]] - source[index_s[0, at]]
            ).astype(BF16)

    def set_hessian(s):
        for p, part in enumerate(three_parts(jnp.transpose(hess[s]))):
            hess_t[pl.ds(p * edge, edge)] = part

    def set_block(s):
        blocks = beta_v[...]
        block_ids = lax.broadcasted_iota(jnp.int32, blocks.shape, 0)
        beta_v[...] = jnp.where(
            block_ids == order_smem[0, s], jnp.broadcast_to(shrunk_all[s], blocks.shape), blocks
        )

    loads[0].wait()
    loads[1].wait()
    products = []
    for m in range(slabs):
        acc = jnp.zeros((SLAB, edge), F32)
        for t in range(SLAB):
            row = beta_v[pl.ds(cols_smem[0, m * SLAB + t], 1), :]
            acc = jnp.where(sub == t, jnp.broadcast_to(row, (SLAB, edge)), acc)
        picked = acc.astype(BF16)
        acc = jnp.zeros((SLAB, edge), F32)
        for t in range(SLAB):
            acc = jnp.where(sub == t, nt_dot(picked, vals[m * SLAB + t]), acc)
        products.append(acc)
    placing = (
        jnp.broadcast_to(ids[0:1, 0:n_tiles], (row_blocks, n_tiles))
        == lax.broadcasted_iota(jnp.int32, (row_blocks, n_tiles), 0)
    ).astype(F32).astype(BF16)
    parts = three_parts(jnp.concatenate(products, axis=0))
    sums = jnp.dot(placing, parts[0], preferred_element_type=F32)
    for part in parts[1:]:
        sums = sums + jnp.dot(placing, part, preferred_element_type=F32)
    partial[...] = sums.reshape(partial.shape)

    pl.semaphore_wait(barrier, n_samp + n_feat - 2)
    n_z = n_feat // 2
    fx, fz = fj // n_z, lax.rem(fj, n_z)
    z_steps = sorted(range(n_z), key=lambda d: -min(d, n_z - d))

    def across_x(k, d):
        return pltpu.make_async_remote_copy(
            src_ref=partial.at[(1 - fx) * n_z + lax.rem(fz + d, n_z)],
            dst_ref=x_recv.at[k],
            send_sem=x_send_sem,
            recv_sem=x_recv_sem.at[k],
            device_id=(si, (1 - fx) * n_z + fz),
            device_id_type=MESH,
        )

    for k, d in enumerate(z_steps):
        across_x(k, d).start()
    for k, d in enumerate(z_steps):
        owner = fx * n_z + lax.rem(fz + d, n_z)
        across_x(k, d).wait_recv()
        both = partial[owner] + x_recv[k]
        if d == 0:
            m_recv[fz] = both
        else:
            m_send[k] = both
            pltpu.make_async_remote_copy(
                src_ref=m_send.at[k],
                dst_ref=m_recv.at[fz],
                send_sem=m_send_sem,
                recv_sem=m_recv_sem,
                device_id=(si, owner),
                device_id_type=MESH,
            ).start()
    loads[2].wait()
    loads[3].wait()
    set_hessian(0)
    index_copy.wait()
    set_prefixes()
    set_dense(0, prefix, dense)
    set_dense(0, prefix_t, dense_t)
    m_others = m_recv.at[pl.ds(0, n_z - 1)]
    pltpu.make_async_copy(m_others, m_others, m_recv_sem).wait()
    margin = tree_sum([m_recv[d] for d in range(n_z)])
    prob = 1.0 / (1.0 + jnp.exp(-margin))
    w_buf[0] = prob * (1.0 - prob)
    r_buf[0] = labels_v[...].astype(F32) - prob

    def shift(buf_src, buf_dst, send_sem, recv_sem):
        return pltpu.make_async_remote_copy(
            src_ref=buf_src,
            dst_ref=buf_dst,
            send_sem=send_sem,
            recv_sem=recv_sem,
            device_id=(si, right),
            device_id_type=MESH,
        )

    shift(w_buf.at[0], w_buf.at[1], w_send_sem, w_recv_sem.at[1]).start()

    peers = sorted(
        ((x, y, c) for x in range(2) for y in range(n_samp // 4) for c in range(2)),
        key=lambda o: -(2 * o[0] + min(o[1], n_samp // 4 - o[1]) + 0.3 * o[2]),
    )[:-1]
    half = n_samp // 2
    my_x, my_y, my_c = si // half, lax.rem(si // 2, n_samp // 4), lax.rem(si, 2)

    def section(s, carry):
        rounded = r_buf[s].astype(BF16)
        picks = jnp.concatenate([mask * rounded for mask in group_is], axis=1)
        local = jnp.zeros((1, edge), F32)
        for grads in two_dots(picks, dense):
            both = grads[:SLAB, :edge] + grads[SLAB:, edge:]
            local = local + jnp.sum(both, axis=0, keepdims=True)
        g_send[s] = local
        for dx, dy, dc in peers:
            peer = (
                lax.rem(my_x + dx, 2) * half
                + lax.rem(my_y + dy, n_samp // 4) * 2
                + lax.rem(my_c + dc, 2)
            )
            pltpu.make_async_remote_copy(
                src_ref=g_send.at[s],
                dst_ref=g_recv.at[s, si],
                send_sem=g_send_sem,
                recv_sem=g_recv_sem.at[s],
                device_id=(peer, fj),
                device_id_type=MESH,
            ).start()
        g_recv[s, si] = local

        @pl.when(s < n_feat - 1)
        def _():
            shift(w_buf.at[s], w_buf.at[s + 1], w_send_sem, w_recv_sem.at[s + 1]).wait_recv()
            set_dense(s + 1, prefix, dense)

        @pl.when(s > 0)
        def _():
            set_block(s - 1)

        @pl.when(s < n_feat - 2)
        def _():
            shift(w_buf.at[s + 1], w_buf.at[s + 2], w_send_sem, w_recv_sem.at[s + 2]).start()

        target = order_smem[0, s]
        current = beta_v[pl.ds(target, 1), :]
        others = g_recv.at[s, pl.ds(0, n_samp - 1)]
        pltpu.make_async_copy(others, others, g_recv_sem.at[s]).wait()
        gradient = tree_sum([g_recv[s, i] for i in range(n_samp)])
        high, middle, low = [
            jnp.broadcast_to(part.astype(F32), (SLAB, edge)) for part in three_parts(gradient)
        ]
        stacked = jnp.where(
            sub == 0, high, jnp.where(sub == 1, middle, jnp.where(sub == 2, low, 0.0))
        ).astype(BF16)
        products = jnp.dot(
            jnp.concatenate([stacked] * 3, axis=1), hess_t[...], preferred_element_type=F32
        )
        moved = current + jnp.sum(products, axis=0, keepdims=True)
        shrunk = jnp.where(moved > L1, moved - L1, jnp.where(moved < -L1, moved + L1, 0.0))
        shrunk_all[s] = shrunk
        change = jnp.broadcast_to(shrunk - current, (SLAB, edge)).astype(BF16)
        spread = jnp.concatenate([row_is[t] * change for t in range(SLAB)], axis=1)
        updated = r_buf[s]
        for halves in two_dots(spread, dense_t):
            landed = jnp.concatenate([halves[:, :edge], halves[:, edge:]], axis=0)
            updated = updated - w_buf[s] * landed
        r_send[s] = updated
        move = shift(r_send.at[s], r_buf.at[s + 1], r_send_sem, r_recv_sem.at[s + 1])
        move.start()

        @pl.when(s < n_feat - 1)
        def _():
            set_hessian(s + 1)
            set_dense(s + 1, prefix_t, dense_t)

        @pl.when(s == n_feat - 1)
        def _():
            set_block(s)
            pltpu.make_async_copy(beta_v, beta_out, load_sem.at[1]).start()

        move.wait_recv()
        return carry

    lax.fori_loop(0, n_feat, section, 0)

    res_copy = pltpu.make_async_copy(r_buf.at[n_feat], res_out, load_sem.at[0])
    res_copy.start()

    pltpu.make_async_copy(x_recv, x_recv, x_send_sem).wait()
    pltpu.make_async_copy(m_others, m_others, m_send_sem).wait()
    sent = g_recv.at[:, pl.ds(0, n_samp - 1)]
    pltpu.make_async_copy(sent, sent, g_send_sem).wait()
    sent_r = r_buf.at[pl.ds(0, n_feat)]
    pltpu.make_async_copy(sent_r, sent_r, r_send_sem).wait()
    sent_w = w_buf.at[pl.ds(0, n_feat - 1)]
    pltpu.make_async_copy(sent_w, sent_w, w_send_sem).wait()
    pltpu.make_async_copy(beta_v, beta_out, load_sem.at[1]).wait()
    res_copy.wait()


def hand_over(beta_ref, res_ref, beta_out, res_out, beta_v, res_v, sems):
    into = [
        pltpu.make_async_copy(beta_ref, beta_v, sems.at[0]),
        pltpu.make_async_copy(res_ref, res_v, sems.at[1]),
    ]
    out = [
        pltpu.make_async_copy(beta_v, beta_out, sems.at[2]),
        pltpu.make_async_copy(res_v, res_out, sems.at[3]),
    ]
    for copy in into:
        copy.start()
    for first, second in zip(into, out):
        first.wait()
        second.start()
    for copy in out:
        copy.wait()


def per_device(n_samp, n_feat, labels, beta, tile_rows, tile_cols, tile_values, block_order, hess_inv):
    n_tiles, edge = tile_values.shape[2], tile_values.shape[-1]
    row_blocks = labels.shape[0] // edge
    feat_blocks = beta.shape[0] // edge
    group = row_blocks // n_feat
    vmem = pl.BlockSpec(memory_space=pltpu.VMEM)
    smem = pl.BlockSpec(memory_space=pltpu.SMEM)
    anywhere = pl.BlockSpec(memory_space=pl.ANY)
    dma = pltpu.SemaphoreType.DMA
    beta_new, residual = pl.pallas_call(
        functools.partial(window_kernel, n_samp, n_feat, n_tiles),
        out_shape=(
            jax.ShapeDtypeStruct((feat_blocks, edge), F32),
            jax.ShapeDtypeStruct((group, edge), F32),
        ),
        in_specs=[vmem, vmem, smem, smem, anywhere, anywhere, anywhere, anywhere],
        out_specs=(anywhere, anywhere),
        scratch_shapes=[
            pltpu.VMEM((group, edge), jnp.int32),
            pltpu.VMEM((feat_blocks, edge), F32),
            pltpu.VMEM((n_tiles, edge, edge), BF16),
            pltpu.VMEM((n_feat, edge, edge), F32),
            pltpu.VMEM((3 * edge, edge), BF16),
            pltpu.VMEM((8, edge), jnp.int32),
            pltpu.VMEM((1, row_blocks + 2 * edge), jnp.int32),
            pltpu.SMEM((1, row_blocks + 2 * edge), jnp.int32),
            pltpu.VMEM((n_tiles + 1, edge, edge), F32),
            pltpu.VMEM((n_tiles + 1, edge, edge), F32),
            pltpu.VMEM((SLAB * edge, group // SLAB * edge), BF16),
            pltpu.VMEM((SLAB * edge, group // SLAB * edge), BF16),
            pltpu.VMEM((n_feat, 1, edge), F32),
            pltpu.VMEM((n_feat, group, edge), F32),
            pltpu.VMEM((n_feat // 2, group, edge), F32),
            pltpu.VMEM((n_feat // 2, group, edge), F32),
            pltpu.VMEM((n_feat // 2, group, edge), F32),
            pltpu.VMEM((n_feat, 1, edge), F32),
            pltpu.VMEM((n_feat, n_samp, 1, edge), F32),
            pltpu.VMEM((n_feat, group, edge), F32),
            pltpu.VMEM((n_feat + 1, group, edge), F32),
            pltpu.VMEM((n_feat, group, edge), F32),
            dma((4,)),
            dma(()),
            dma(()),
            dma((n_feat // 2,)),
            dma(()),
            dma(()),
            dma(()),
            dma((n_feat,)),
            dma(()),
            dma((n_feat + 1,)),
            dma(()),
            dma((n_feat,)),
        ],
        compiler_params=pltpu.CompilerParams(
            collective_id=0, has_side_effects=True
        ),
    )(
        tile_rows.reshape(1, n_tiles),
        tile_cols.reshape(1, n_tiles),
        tile_cols.reshape(1, n_tiles),
        block_order,
        labels.reshape(row_blocks, edge),
        beta.reshape(feat_blocks, edge),
        tile_values.reshape(n_tiles, edge, edge),
        hess_inv.reshape(n_feat, edge, edge),
    )
    beta_new, residual = pl.pallas_call(
        hand_over,
        out_shape=(
            jax.ShapeDtypeStruct((feat_blocks, edge), F32),
            jax.ShapeDtypeStruct((group, edge), F32),
        ),
        in_specs=[anywhere, anywhere],
        out_specs=(anywhere, anywhere),
        scratch_shapes=[
            pltpu.VMEM((feat_blocks, edge), F32),
            pltpu.VMEM((group, edge), F32),
            dma((4,)),
        ],
    )(beta_new, residual)
    return beta_new.reshape(-1), residual.reshape(-1)


def solution(mesh):
    placed = (
        P("samp"),
        P("feat"),
        P("samp", "feat", None),
        P("samp", "feat", None),
        P("samp", "feat", None, None, None),
        P("feat", None),
        P("feat", None, None, None),
    )
    return jax.shard_map(
        functools.partial(per_device, mesh.shape["samp"], mesh.shape["feat"]),
        mesh=mesh,
        in_specs=placed,
        out_specs=(P("feat"), P(("samp", "feat"))),
        check_vma=False,
    )
```
